32 devices in a mesh: sect: 2 (over x), seq: 4 (over y, core), dp: 4 (over z).
Axes of the slice: x: 2, y: 2, z: 4, core: 2. Of those that a mesh axis runs over, the one named last changes fastest.
Arguments:
- query_tiles: bfloat16 [4, 8, 128, 2048], P('dp', None, 'sect', 'seq'), may hold values from -6 to 6
- key_tiles: bfloat16 [4, 8, 128, 2048], P('dp', None, 'sect', 'seq'), may hold values from -6 to 6
- value_tiles: bfloat16 [4, 8, 128, 2048], P('dp', None, 'sect', 'seq'), may hold values from -6 to 6
- text_keys: bfloat16 [8, 256, 2048], P(('sect', 'dp'), 'seq'), may hold values from -6 to 6
- text_values: bfloat16 [8, 256, 2048], P(('sect', 'dp'), 'seq'), may hold values from -6 to 6
- text_lengths: int32 [8], P(('sect', 'dp')), may hold values from 32 to 256, as said below
- tile_place: int32 [4], replicated, may hold values from 0 to 3, each once
Outputs:
- attended: bfloat16 [8, 512, 2048], P(('sect', 'dp'), 'seq')
The draws below stay inside these ranges and needn't reach their ends.
Inputs may be any that keep to these rules, and one draw needn't show every extreme that they name: `tile_place`: each spatial position is held by exactly one tile slot. `text_lengths`: the live text tokens of a clip are its first rows; some clip fills all 256 slots.
All inputs are finite; a program needn't handle non-finite values.
Results may differ from the reference program's by a relative error of at most 0.0031.
Values may be sent and summed in bfloat16 or wider, within the bound.
A program may use at most 64 MiB of HBM per device.

```python
import math
import jax
import jax.numpy as jnp
from jax import lax

HD = 128
HEADS = 16
TEXT = 256
TILES = 4
BLOCKS = 4
CLIPS = 8
TILE_ROWS = 32
TILE_SEQ = 128
TOKENS = 512
QW = 2048


def joint_draw(key):
    base = jax.random.fold_in(key, 11)
    key_query, key_keys = jax.random.split(base, 2)
    full_shape = (TILES, CLIPS, TILE_SEQ, HEADS * HD)
    queries = 1.6 * jax.random.truncated_normal(key_query, -3.75, 3.75, full_shape, jnp.float32)
    keys_all = 1.6 * jax.random.truncated_normal(key_keys, -3.75, 3.75, full_shape, jnp.float32)
    return (queries, keys_all)


def draw_query_tiles(key, part):
    return joint_draw(key)[0].astype(jnp.bfloat16)


def draw_key_tiles(key, part):
    return joint_draw(key)[1].astype(jnp.bfloat16)


def draw_text_lengths(key, part):
    base = jax.random.fold_in(key, 23)
    first_key, second_key = jax.random.split(base, 2)
    lengths = jax.random.randint(first_key, (CLIPS,), TEXT // 8, TEXT + 1).astype(jnp.int32)
    filled = jax.random.randint(second_key, (), 0, CLIPS)
    return lengths.at[filled].set(TEXT).astype(jnp.int32)


def steps_of(stream_key, dims, shards, low, largest):
    level = 1.0
    for position, shards_of in shards:
        draws = jax.random.uniform(jax.random.fold_in(jax.random.fold_in(stream_key, 6), position), (shards_of,), jnp.float32, low / len(shards), largest / len(shards))
        level = level * jnp.repeat(jnp.exp(draws), dims[position] // shards_of).reshape((-1,) + (1,) * (len(dims) - 1 - position))
    return level


def scatter_about(key, shape, deviation, reach, cuts=(), kind=jnp.bfloat16):
    drawn = deviation * jax.random.normal(key, shape, jnp.float32)
    if cuts:
        drawn = drawn * steps_of(key, shape, cuts, -0.22, 0.18)
    return jnp.clip(drawn, -reach, reach).astype(kind)


def setup_inputs(seed: int = 0) -> dict:
    key_of = jax.random.split(jax.random.key(seed), 8)
    return {
        "query_tiles": draw_query_tiles(jax.random.fold_in(key_of[7], 71), 0),
        "key_tiles": draw_key_tiles(jax.random.fold_in(key_of[7], 71), 0),
        "value_tiles": scatter_about(key_of[2], (TILES, CLIPS, TILE_SEQ, QW), 1.0, 6.0, ((0, 4), (2, 2), (3, 4))),
        "text_keys": scatter_about(key_of[3], (CLIPS, TEXT, QW), 1.6, 6.0, ((0, 8), (1, 4))),
        "text_values": scatter_about(key_of[4], (CLIPS, TEXT, QW), 1.0, 6.0, ((0, 8), (1, 4))),
        "text_lengths": draw_text_lengths(jax.random.fold_in(key_of[7], 71), 0),
        "tile_place": jax.random.permutation(key_of[6], TILES).astype(jnp.int32),
    }


def reference(query_tiles, key_tiles, value_tiles, text_keys, text_values, text_lengths, tile_place):
    inverse = jnp.argsort(tile_place).astype(jnp.int32)

    def assemble(tiles):
        placed = jnp.take(tiles, inverse, axis=0)
        placed = placed.reshape(TILES, CLIPS, BLOCKS, TILE_ROWS, HEADS, HD)
        placed = jnp.transpose(placed, (1, 2, 0, 3, 4, 5))
        return placed.reshape(CLIPS, TOKENS, HEADS, HD)
    video_queries = assemble(query_tiles)
    video_keys = assemble(key_tiles)
    video_values = assemble(value_tiles)
    text_key_rows = text_keys.reshape(CLIPS, TEXT, HEADS, HD)
    text_value_rows = text_values.reshape(CLIPS, TEXT, HEADS, HD)
    score_scale = 1.0 / math.sqrt(HD)

    def one_clip(operands):
        queries, keys_video, values_video, keys_text, values_text, length = operands
        all_keys = jnp.concatenate([keys_video, keys_text], 0).astype(jnp.float32)
        all_values = jnp.concatenate([values_video, values_text], 0).astype(jnp.float32)
        live_mask = jnp.concatenate([jnp.ones((TOKENS,), bool), jnp.arange(TEXT, dtype=jnp.int32) < length])
        scores = jnp.einsum('qhd,khd->hqk', queries.astype(jnp.float32), all_keys) * score_scale
        scores = jnp.where(live_mask[None, None, :], scores, -jnp.inf)
        row_max = lax.optimization_barrier(jnp.max(scores, axis=-1, keepdims=True))
        exponentials = jnp.exp(scores - row_max)
        denominators = lax.optimization_barrier(jnp.sum(exponentials, axis=-1))
        weights = lax.optimization_barrier(exponentials.astype(jnp.bfloat16))
        mixed = jnp.einsum('hqk,khd->qhd', weights.astype(jnp.float32), all_values)
        return (mixed / jnp.transpose(denominators)[:, :, None]).astype(jnp.bfloat16)
    attended = lax.map(one_clip, (video_queries, video_keys, video_values, text_key_rows, text_value_rows, text_lengths))
    return attended.reshape(CLIPS, TOKENS, HEADS * HD)
```

```python
import functools
import math

import jax
import jax.numpy as jnp
from jax import lax
from jax.experimental import pallas as pl
from jax.experimental.pallas import tpu as pltpu
from jax.sharding import PartitionSpec as P

HD = 128


def attend(queries_flat, keys_video, values_video, keys_text, values_text, length):
    query_rows, head_width = queries_flat.shape
    head_count = head_width // HD
    score_scale = 1.0 / math.sqrt(HD)
    keys_video = keys_video.reshape(-1, head_count, HD)
    values_video = values_video.reshape(-1, head_count, HD)
    keys_text = keys_text.reshape(-1, head_count, HD)
    values_text = values_text.reshape(-1, head_count, HD)
    live_mask = jnp.arange(keys_text.shape[0], dtype=jnp.int32) < length
    block_rows = math.gcd(query_rows, 512)

    def one_block(query_block):
        score_video = (
            jnp.einsum("qhd,khd->hqk", query_block, keys_video, preferred_element_type=jnp.float32)
            * score_scale
        )
        score_text = (
            jnp.einsum("qhd,khd->hqk", query_block, keys_text, preferred_element_type=jnp.float32)
            * score_scale
        )
        score_text = jnp.where(live_mask[None, None, :], score_text, -jnp.inf)
        row_max = jnp.maximum(jnp.max(score_video, axis=-1), jnp.max(score_text, axis=-1))[
            ..., None
        ]
        expo_video = jnp.exp(score_video - row_max)
        expo_text = jnp.exp(score_text - row_max)
        denominators = jnp.sum(expo_video, axis=-1) + jnp.sum(expo_text, axis=-1)
        mixed = jnp.einsum(
            "hqk,khd->qhd",
            expo_video.astype(jnp.bfloat16),
            values_video,
            preferred_element_type=jnp.float32,
        )
        mixed = mixed + jnp.einsum(
            "hqk,khd->qhd",
            expo_text.astype(jnp.bfloat16),
            values_text,
            preferred_element_type=jnp.float32,
        )
        return (mixed / jnp.transpose(denominators)[:, :, None]).astype(jnp.bfloat16)

    blocks = queries_flat.reshape(query_rows // block_rows, block_rows, head_count, HD)
    return lax.map(one_block, blocks).reshape(query_rows, head_width)


def shards(query_tiles, key_tiles, value_tiles, text_keys, text_values, text_lengths, tile_place):
    tile_count = lax.axis_size("dp")
    sect_count = lax.axis_size("sect")
    part_rows = query_tiles.shape[2]
    head_width = query_tiles.shape[3]
    tile_seq = part_rows * sect_count

    def regroup(piece):
        return piece.reshape(1, sect_count, tile_count, part_rows, head_width)

    relayed = (
        lax.all_to_all(
            lax.all_to_all(regroup(query_tiles), "sect", split_axis=1, concat_axis=3, tiled=True),
            "dp",
            split_axis=2,
            concat_axis=0,
            tiled=True,
        ),
        lax.all_to_all(
            lax.all_to_all(regroup(key_tiles), "sect", split_axis=1, concat_axis=3, tiled=True),
            "dp",
            split_axis=2,
            concat_axis=0,
            tiled=True,
        ),
        lax.all_to_all(
            lax.all_to_all(regroup(value_tiles), "sect", split_axis=1, concat_axis=3, tiled=True),
            "dp",
            split_axis=2,
            concat_axis=0,
            tiled=True,
        ),
    )
    spatial_order = jnp.argsort(tile_place)
    seq_count = lax.axis_size("seq")
    tile_rows = tile_seq // seq_count

    def arrange(piece):
        grid = piece.reshape(tile_count, seq_count, tile_rows, head_width)
        placed = jnp.take(grid, spatial_order, axis=0)
        placed = jnp.transpose(placed, (1, 0, 2, 3))
        return placed.reshape(seq_count * tile_count * tile_rows, head_width)

    video_queries = arrange(relayed[0])
    video_keys = arrange(relayed[1])
    video_values = arrange(relayed[2])
    keys_text, values_text = (
        lax.all_to_all(text_keys[0], "seq", split_axis=1, concat_axis=0, tiled=True),
        lax.all_to_all(text_values[0], "seq", split_axis=1, concat_axis=0, tiled=True),
    )
    attended_heads = attend(
        video_queries, video_keys, video_values, keys_text, values_text, text_lengths[0]
    )
    attended = lax.all_to_all(attended_heads, "seq", split_axis=0, concat_axis=1, tiled=True)
    return attended[None]


def peer_order(sect_count, tile_count):
    half = tile_count // 2
    steps = sorted(range(tile_count), key=lambda step: abs(step - half))
    pairs = [(o, step) for step in steps for o in reversed(range(sect_count))]
    return [pair for pair in pairs if pair != (0, 0)]


def relay_kernel(
    sizes,
    q_ref, k_ref, v_ref, tk_ref, tv_ref, len_ref,
    out_ref,
    buf, tbuf, obuf,
    send_sem, recv_sem, text_send, text_recv, out_send, out_recv,
):
    sect_count, seq_count, tile_count, heads, part_blocks, rows, text_part = sizes
    me_s, me_q, me_d = lax.axis_index("sect"), lax.axis_index("seq"), lax.axis_index("dp")
    mesh_ids = pl.DeviceIdType.MESH
    width = heads * HD
    order = peer_order(sect_count, tile_count)
    block_rows = tile_count * rows
    text_rows = text_part * seq_count

    def group_peer(offset):
        return lax.rem(me_s + offset[0], sect_count), lax.rem(me_d + offset[1], tile_count)

    barrier = pltpu.get_barrier_semaphore()
    for offset in order:
        to_s, to_d = group_peer(offset)
        pl.semaphore_signal(barrier, inc=1, device_id={"sect": to_s, "dp": to_d}, device_id_type=mesh_ids)
    for step in range(1, seq_count):
        to_q = lax.rem(me_q + step, seq_count)
        pl.semaphore_signal(barrier, inc=1, device_id={"seq": to_q}, device_id_type=mesh_ids)

    sources = (q_ref, k_ref, v_ref)
    texts = (tk_ref, tv_ref)

    def piece(number, clip, c):
        return sources[number].at[clip, :, :, pl.ds(c * HD, HD)]

    def landing(number, c):
        return buf.at[c, number, pl.ds(me_s * part_blocks, part_blocks), me_d]

    mine = me_s * tile_count + me_d
    for c in range(heads):
        for number in range(3):
            pltpu.make_async_copy(piece(number, mine, c), landing(number, c), recv_sem.at[c]).start()
    my_text = pl.ds(me_q * text_part, text_part)
    for number in range(2):
        pltpu.make_async_copy(
            texts[number].at[:, pl.ds(pl.multiple_of(me_q * width, HD), width)],
            tbuf.at[number, my_text],
            text_recv,
        ).start()

    pl.semaphore_wait(barrier, len(order) + seq_count - 1)

    def send_chunk(c):
        for offset in order:
            to_s, to_d = group_peer(offset)
            for number in range(3):
                pltpu.make_async_remote_copy(
                    src_ref=piece(number, to_s * tile_count + to_d, c),
                    dst_ref=landing(number, c),
                    send_sem=send_sem.at[number],
                    recv_sem=recv_sem.at[c],
                    device_id={"sect": to_s, "dp": to_d},
                    device_id_type=mesh_ids,
                ).start()

    send_chunk(0)
    for step in range(1, seq_count):
        to_q = lax.rem(me_q + step, seq_count)
        for number in range(2):
            pltpu.make_async_remote_copy(
                src_ref=texts[number].at[:, pl.ds(pl.multiple_of(to_q * width, HD), width)],
                dst_ref=tbuf.at[number, my_text],
                send_sem=text_send,
                recv_sem=text_recv,
                device_id={"seq": to_q},
                device_id_type=mesh_ids,
            ).start()
    for c in range(1, heads):
        send_chunk(c)

    factor = math.log2(math.e) / math.sqrt(HD)
    pltpu.make_async_copy(tbuf, tbuf, text_recv).wait()
    live = lax.broadcasted_iota(jnp.int32, (1, text_rows), 1) < len_ref[0]
    contract_last = (((1,), (1,)), ((), ()))
    for c in range(heads):
        pltpu.make_async_copy(buf.at[c], buf.at[c], recv_sem.at[c]).wait()
        columns = slice(c * HD, (c + 1) * HD)
        keys = buf[c, 1].reshape(seq_count * block_rows, HD)
        values = buf[c, 2].reshape(seq_count * block_rows, HD)
        keys_text = tbuf[0, :, columns]
        values_text = tbuf[1, :, columns]
        for step in list(range(1, seq_count)) + [0]:
            to_q = lax.rem(me_q + step, seq_count)
            queries = buf[c, 0, to_q].reshape(block_rows, HD)
            video = lax.dot_general(queries, keys, contract_last, preferred_element_type=jnp.float32)
            text = lax.dot_general(queries, keys_text, contract_last, preferred_element_type=jnp.float32)
            text = jnp.where(live, text, -jnp.inf)
            top = jnp.maximum(jnp.max(video, axis=1, keepdims=True), jnp.max(text, axis=1, keepdims=True))
            video = jnp.exp2((video - top) * factor)
            text = jnp.exp2((text - top) * factor)
            total = jnp.sum(video, axis=1, keepdims=True) + jnp.sum(text, axis=1, keepdims=True)
            mixed = jnp.dot(video.astype(jnp.bfloat16), values, preferred_element_type=jnp.float32)
            mixed = mixed + jnp.dot(
                text.astype(jnp.bfloat16), values_text, preferred_element_type=jnp.float32
            )
            obuf[c, step] = (mixed / total).astype(jnp.bfloat16)
            place = out_ref.at[:, pl.ds(pl.multiple_of((me_q * heads + c) * HD, HD), HD)]
            if step == 0:
                pltpu.make_async_copy(obuf.at[c, step], place, out_recv).start()
            else:
                pltpu.make_async_remote_copy(
                    src_ref=obuf.at[c, step],
                    dst_ref=place,
                    send_sem=out_send,
                    recv_sem=out_recv,
                    device_id={"seq": to_q},
                    device_id_type=mesh_ids,
                ).start()

    for number in range(3):
        view = sources[number].at[pl.ds(0, len(order))]
        pltpu.make_async_copy(view, view, send_sem.at[number]).wait()
    text_view = tbuf.at[:, pl.ds(0, text_part * (seq_count - 1))]
    pltpu.make_async_copy(text_view, text_view, text_send).wait()
    out_view = obuf.at[:, pl.ds(1, seq_count - 1)]
    pltpu.make_async_copy(out_view, out_view, out_send).wait()
    pltpu.make_async_copy(out_ref, out_ref, out_recv).wait()


def place_kernel(place_ref, rows_ref, out_ref):
    out_ref[...] = rows_ref[...]


def fused_shards(query_tiles, key_tiles, value_tiles, text_keys, text_values, text_lengths, tile_place):
    sect_count, seq_count, tile_count = (lax.axis_size(name) for name in ("sect", "seq", "dp"))
    clips, part_rows, width = query_tiles.shape[1:]
    rows = part_rows * sect_count // seq_count
    heads = width // HD
    part_blocks = part_rows // rows
    text_part, all_width = text_keys.shape[1:]
    out_rows = tile_count * rows
    sizes = (sect_count, seq_count, tile_count, heads, part_blocks, rows, text_part)
    hbm = pl.BlockSpec(memory_space=pl.ANY)

    def blocks(piece):
        return piece.reshape(clips, part_blocks, rows, width)

    gathered = pl.pallas_call(
        functools.partial(relay_kernel, sizes),
        out_shape=jax.ShapeDtypeStruct((out_rows, all_width), jnp.bfloat16),
        in_specs=[hbm] * 5 + [pl.BlockSpec(memory_space=pltpu.SMEM)],
        out_specs=hbm,
        scratch_shapes=[
            pltpu.VMEM((heads, 3, seq_count, tile_count, rows, HD), jnp.bfloat16),
            pltpu.VMEM((2, text_part * seq_count, width), jnp.bfloat16),
            pltpu.VMEM((heads, seq_count, out_rows, HD), jnp.bfloat16),
            pltpu.SemaphoreType.DMA((3,)),
            pltpu.SemaphoreType.DMA((heads,)),
            pltpu.SemaphoreType.DMA,
            pltpu.SemaphoreType.DMA,
            pltpu.SemaphoreType.DMA,
            pltpu.SemaphoreType.DMA,
        ],
        compiler_params=pltpu.CompilerParams(collective_id=0, has_side_effects=True),
    )(
        blocks(query_tiles),
        blocks(key_tiles),
        blocks(value_tiles),
        text_keys[0],
        text_values[0],
        text_lengths,
    )
    attended = pl.pallas_call(
        place_kernel,
        grid_spec=pltpu.PrefetchScalarGridSpec(
            num_scalar_prefetch=1,
            grid=(tile_count,),
            in_specs=[pl.BlockSpec((rows, all_width), lambda t, place: (t, 0))],
            out_specs=pl.BlockSpec((rows, all_width), lambda t, place: (place[t], 0)),
        ),
        out_shape=jax.ShapeDtypeStruct((out_rows, all_width), jnp.bfloat16),
    )(tile_place, gathered)
    return attended[None]


def solution(mesh):
    in_specs = (
        P("dp", None, "sect", "seq"),
        P("dp", None, "sect", "seq"),
        P("dp", None, "sect", "seq"),
        P(("sect", "dp"), "seq", None),
        P(("sect", "dp"), "seq", None),
        P(("sect", "dp")),
        P(),
    )
    out_specs = P(("sect", "dp"), "seq", None)

    def pick(*operands):
        rows = operands[0].shape[2] * mesh.shape["sect"] // mesh.shape["seq"]
        return (shards if rows % 16 else fused_shards)(*operands)

    return jax.shard_map(pick, mesh=mesh, in_specs=in_specs, out_specs=out_specs, check_vma=False)
```

```python
import functools
import math

import jax
import jax.numpy as jnp
from jax import lax
from jax.experimental import pallas as pl
from jax.experimental.pallas import tpu as pltpu
from jax.sharding import PartitionSpec as P

HD = 128


def attend(queries_flat, keys_video, values_video, keys_text, values_text, length):
    query_rows, head_width = queries_flat.shape
    head_count = head_width // HD
    score_scale = 1.0 / math.sqrt(HD)
    keys_video = keys_video.reshape(-1, head_count, HD)
    values_video = values_video.reshape(-1, head_count, HD)
    keys_text = keys_text.reshape(-1, head_count, HD)
    values_text = values_text.reshape(-1, head_count, HD)
    live_mask = jnp.arange(keys_text.shape[0], dtype=jnp.int32) < length
    block_rows = math.gcd(query_rows, 512)

    def one_block(query_block):
        score_video = (
            jnp.einsum("qhd,khd->hqk", query_block, keys_video, preferred_element_type=jnp.float32)
            * score_scale
        )
        score_text = (
            jnp.einsum("qhd,khd->hqk", query_block, keys_text, preferred_element_type=jnp.float32)
            * score_scale
        )
        score_text = jnp.where(live_mask[None, None, :], score_text, -jnp.inf)
        row_max = jnp.maximum(jnp.max(score_video, axis=-1), jnp.max(score_text, axis=-1))[
            ..., None
        ]
        expo_video = jnp.exp(score_video - row_max)
        expo_text = jnp.exp(score_text - row_max)
        denominators = jnp.sum(expo_video, axis=-1) + jnp.sum(expo_text, axis=-1)
        mixed = jnp.einsum(
            "hqk,khd->qhd",
            expo_video.astype(jnp.bfloat16),
            values_video,
            preferred_element_type=jnp.float32,
        )
        mixed = mixed + jnp.einsum(
            "hqk,khd->qhd",
            expo_text.astype(jnp.bfloat16),
            values_text,
            preferred_element_type=jnp.float32,
        )
        return (mixed / jnp.transpose(denominators)[:, :, None]).astype(jnp.bfloat16)

    blocks = queries_flat.reshape(query_rows // block_rows, block_rows, head_count, HD)
    return lax.map(one_block, blocks).reshape(query_rows, head_width)


def shards(query_tiles, key_tiles, value_tiles, text_keys, text_values, text_lengths, tile_place):
    tile_count = lax.axis_size("dp")
    sect_count = lax.axis_size("sect")
    part_rows = query_tiles.shape[2]
    head_width = query_tiles.shape[3]
    tile_seq = part_rows * sect_count

    def regroup(piece):
        return piece.reshape(1, sect_count, tile_count, part_rows, head_width)

    relayed = (
        lax.all_to_all(
            lax.all_to_all(regroup(query_tiles), "sect", split_axis=1, concat_axis=3, tiled=True),
            "dp",
            split_axis=2,
            concat_axis=0,
            tiled=True,
        ),
        lax.all_to_all(
            lax.all_to_all(regroup(key_tiles), "sect", split_axis=1, concat_axis=3, tiled=True),
            "dp",
            split_axis=2,
            concat_axis=0,
            tiled=True,
        ),
        lax.all_to_all(
            lax.all_to_all(regroup(value_tiles), "sect", split_axis=1, concat_axis=3, tiled=True),
            "dp",
            split_axis=2,
            concat_axis=0,
            tiled=True,
        ),
    )
    spatial_order = jnp.argsort(tile_place)
    seq_count = lax.axis_size("seq")
    tile_rows = tile_seq // seq_count

    def arrange(piece):
        grid = piece.reshape(tile_count, seq_count, tile_rows, head_width)
        placed = jnp.take(grid, spatial_order, axis=0)
        placed = jnp.transpose(placed, (1, 0, 2, 3))
        return placed.reshape(seq_count * tile_count * tile_rows, head_width)

    video_queries = arrange(relayed[0])
    video_keys = arrange(relayed[1])
    video_values = arrange(relayed[2])
    keys_text, values_text = (
        lax.all_to_all(text_keys[0], "seq", split_axis=1, concat_axis=0, tiled=True),
        lax.all_to_all(text_values[0], "seq", split_axis=1, concat_axis=0, tiled=True),
    )
    attended_heads = attend(
        video_queries, video_keys, video_values, keys_text, values_text, text_lengths[0]
    )
    attended = lax.all_to_all(attended_heads, "seq", split_axis=0, concat_axis=1, tiled=True)
    return attended[None]


def peer_order(sect_count, tile_count):
    half = tile_count // 2
    steps = sorted(range(tile_count), key=lambda step: abs(step - half))
    pairs = [(o, step) for step in steps for o in reversed(range(sect_count))]
    pairs = [pair for pair in pairs if pair != (0, 0)]
    return pairs


def relay_kernel(
    sizes,
    q_ref, k_ref, v_ref, tk_ref, tv_ref, len_in, place_in,
    out_ref,
    qbufs, kbuf, vbuf, tbuf, pbuf, dbuf, obuf, len_ref, place_ref,
    send_sem, recv_sem, text_send, text_recv, out_send, out_recv, scalar_sems,
):
    sect_count, seq_count, tile_count, heads, part_blocks, rows, text_part = sizes
    me_s, me_q, me_d = lax.axis_index("sect"), lax.axis_index("seq"), lax.axis_index("dp")
    mesh_ids = pl.DeviceIdType.MESH
    width = heads * HD
    order = peer_order(sect_count, tile_count)
    block_rows = tile_count * rows
    text_rows = text_part * seq_count

    def group_peer(offset):
        return lax.rem(me_s + offset[0], sect_count), lax.rem(me_d + offset[1], tile_count)

    scalars = (
        pltpu.make_async_copy(len_in, len_ref, scalar_sems.at[0]),
        pltpu.make_async_copy(place_in, place_ref, scalar_sems.at[1]),
    )
    for copy in scalars:
        copy.start()
    barrier = pltpu.get_barrier_semaphore()
    for offset in order:
        to_s, to_d = group_peer(offset)
        pl.semaphore_signal(barrier, inc=1, device_id={"sect": to_s, "dp": to_d}, device_id_type=mesh_ids)
    for step in range(1, seq_count):
        to_q = lax.rem(me_q + step, seq_count)
        pl.semaphore_signal(barrier, inc=1, device_id={"seq": to_q}, device_id_type=mesh_ids)

    sources = (q_ref, k_ref, v_ref)
    texts = (tk_ref, tv_ref)

    def piece(number, clip, c):
        return sources[number].at[clip, :, :, pl.ds(c * HD, HD)]

    def landing(number, c):
        blocks = pl.ds(me_s * part_blocks, part_blocks)
        return (qbufs[c], kbuf.at[c], vbuf.at[c])[number].at[blocks, me_d]

    def arrival(number, c):
        return recv_sem.at[number, c]

    mine = me_s * tile_count + me_d
    for c in range(heads):
        for number in range(3):
            pltpu.make_async_copy(piece(number, mine, c), landing(number, c), arrival(number, c)).start()
    my_text = pl.ds(me_q * text_part, text_part)
    for number in range(2):
        pltpu.make_async_copy(
            texts[number].at[:, pl.ds(pl.multiple_of(me_q * width, HD), width)],
            tbuf.at[number, my_text],
            text_recv,
        ).start()

    pl.semaphore_wait(barrier, len(order) + seq_count - 1)

    def send_chunk(c):
        for offset in order:
            to_s, to_d = group_peer(offset)
            for number in range(3):
                pltpu.make_async_remote_copy(
                    src_ref=piece(number, to_s * tile_count + to_d, c),
                    dst_ref=landing(number, c),
                    send_sem=send_sem.at[number],
                    recv_sem=arrival(number, c),
                    device_id={"sect": to_s, "dp": to_d},
                    device_id_type=mesh_ids,
                ).start()

    send_chunk(0)
    for step in range(1, seq_count):
        to_q = lax.rem(me_q + step, seq_count)
        for number in range(2):
            pltpu.make_async_remote_copy(
                src_ref=texts[number].at[:, pl.ds(pl.multiple_of(to_q * width, HD), width)],
                dst_ref=tbuf.at[number, my_text],
                send_sem=text_send,
                recv_sem=text_recv,
                device_id={"seq": to_q},
                device_id_type=mesh_ids,
            ).start()
    for c in range(1, heads):
        send_chunk(c)

    factor = math.log2(math.e) / math.sqrt(HD)
    pltpu.make_async_copy(tbuf, tbuf, text_recv).wait()
    for copy in scalars:
        copy.wait()
    live = lax.broadcasted_iota(jnp.int32, (1, text_rows), 1) < len_ref[0]
    holders = []
    for place in range(tile_count):
        holder = jnp.int32(0)
        for slot in range(1, tile_count):
            holder = jnp.where(place_ref[slot] == place, slot, holder)
        holders.append(holder)
    contract_last = (((1,), (1,)), ((), ()))
    for c in range(heads):
        pltpu.make_async_copy(qbufs[c], qbufs[c], arrival(0, c)).wait()
        pltpu.make_async_copy(kbuf.at[c], kbuf.at[c], arrival(1, c)).wait()
        columns = slice(c * HD, (c + 1) * HD)
        keys = kbuf[c].reshape(seq_count * block_rows, HD)
        keys_text = tbuf[0, :, columns]
        steps = list(range(1, seq_count)) + [0]
        for step in steps:
            to_q = lax.rem(me_q + step, seq_count)
            queries = jnp.concatenate([qbufs[c][to_q, slot] for slot in holders], axis=0)
            video = lax.dot_general(queries, keys, contract_last, preferred_element_type=jnp.float32)
            text = lax.dot_general(queries, keys_text, contract_last, preferred_element_type=jnp.float32)
            text = jnp.where(live, text, -jnp.inf)
            top = jnp.maximum(jnp.max(video, axis=1, keepdims=True), jnp.max(text, axis=1, keepdims=True))
            video = jnp.exp2((video - top) * factor)
            text = jnp.exp2((text - top) * factor)
            total = jnp.sum(video, axis=1, keepdims=True) + jnp.sum(text, axis=1, keepdims=True)
            pbuf[step, :, : video.shape[1]] = video.astype(jnp.bfloat16)
            pbuf[step, :, video.shape[1] :] = text.astype(jnp.bfloat16)
            dbuf[step] = jnp.broadcast_to(total, (block_rows, HD))
        pltpu.make_async_copy(vbuf.at[c], vbuf.at[c], arrival(2, c)).wait()
        values = jnp.concatenate(
            [vbuf[c].reshape(seq_count * block_rows, HD), tbuf[1, :, columns]], axis=0
        )
        for step in steps:
            to_q = lax.rem(me_q + step, seq_count)
            mixed = jnp.dot(pbuf[step], values, preferred_element_type=jnp.float32)
            obuf[c, step] = (mixed / dbuf[step]).astype(jnp.bfloat16)
            place = out_ref.at[:, pl.ds(pl.multiple_of((me_q * heads + c) * HD, HD), HD)]
            if step == 0:
                pltpu.make_async_copy(obuf.at[c, step], place, out_recv).start()
            else:
                pltpu.make_async_remote_copy(
                    src_ref=obuf.at[c, step],
                    dst_ref=place,
                    send_sem=out_send,
                    recv_sem=out_recv,
                    device_id={"seq": to_q},
                    device_id_type=mesh_ids,
                ).start()

    for number in range(3):
        view = sources[number].at[pl.ds(0, len(order))]
        pltpu.make_async_copy(view, view, send_sem.at[number]).wait()
    text_view = tbuf.at[:, pl.ds(0, text_part * (seq_count - 1))]
    pltpu.make_async_copy(text_view, text_view, text_send).wait()
    out_view = obuf.at[:, pl.ds(1, seq_count - 1)]
    pltpu.make_async_copy(out_view, out_view, out_send).wait()
    pltpu.make_async_copy(out_ref, out_ref, out_recv).wait()


def fused_shards(query_tiles, key_tiles, value_tiles, text_keys, text_values, text_lengths, tile_place):
    sect_count, seq_count, tile_count = (lax.axis_size(name) for name in ("sect", "seq", "dp"))
    clips, part_rows, width = query_tiles.shape[1:]
    rows = part_rows * sect_count // seq_count
    heads = width // HD
    part_blocks = part_rows // rows
    text_part, all_width = text_keys.shape[1:]
    out_rows = tile_count * rows
    sizes = (sect_count, seq_count, tile_count, heads, part_blocks, rows, text_part)
    hbm = pl.BlockSpec(memory_space=pl.ANY)

    def blocks(piece):
        return piece.reshape(clips, part_blocks, rows, width)

    gathered = pl.pallas_call(
        functools.partial(relay_kernel, sizes),
        out_shape=pltpu.VMEM((out_rows, all_width), jnp.bfloat16),
        in_specs=[hbm] * 7,
        out_specs=pl.BlockSpec(memory_space=pltpu.VMEM),
        scratch_shapes=[
            [pltpu.VMEM((seq_count, tile_count, rows, HD), jnp.bfloat16)] * heads,
            pltpu.VMEM((heads, seq_count, tile_count, rows, HD), jnp.bfloat16),
            pltpu.VMEM((heads, seq_count, tile_count, rows, HD), jnp.bfloat16),
            pltpu.VMEM((2, text_part * seq_count, width), jnp.bfloat16),
            pltpu.VMEM((seq_count, out_rows, seq_count * (out_rows + text_part)), jnp.bfloat16),
            pltpu.VMEM((seq_count, out_rows, HD), jnp.float32),
            pltpu.VMEM((heads, seq_count, out_rows, HD), jnp.bfloat16),
            pltpu.SMEM((1,), jnp.int32),
            pltpu.SMEM((tile_count,), jnp.int32),
            pltpu.SemaphoreType.DMA((3,)),
            pltpu.SemaphoreType.DMA((3, heads)),
            pltpu.SemaphoreType.DMA,
            pltpu.SemaphoreType.DMA,
            pltpu.SemaphoreType.DMA,
            pltpu.SemaphoreType.DMA,
            pltpu.SemaphoreType.DMA((2,)),
        ],
        compiler_params=pltpu.CompilerParams(collective_id=0, has_side_effects=True),
    )(
        blocks(query_tiles),
        blocks(key_tiles),
        blocks(value_tiles),
        text_keys[0],
        text_values[0],
        text_lengths,
        tile_place,
    )
    return gathered[None]


def solution(mesh):
    in_specs = (
        P("dp", None, "sect", "seq"),
        P("dp", None, "sect", "seq"),
        P("dp", None, "sect", "seq"),
        P(("sect", "dp"), "seq", None),
        P(("sect", "dp"), "seq", None),
        P(("sect", "dp")),
        P(),
    )
    out_specs = P(("sect", "dp"), "seq", None)

    def pick(*operands):
        rows = operands[0].shape[2] * mesh.shape["sect"] // mesh.shape["seq"]
        return (shards if rows % 16 else fused_shards)(*operands)

    return jax.shard_map(pick, mesh=mesh, in_specs=in_specs, out_specs=out_specs, check_vma=False)
```
